32 devices in a mesh: range: 8 (over y, x, core), pulse: 4 (over z).
Axes of the slice: x: 2, y: 2, z: 4, core: 2. Of those that a mesh axis runs over, the one named last changes fastest.
Arguments:
- samples: float32 [8192, 2048], P('range', 'pulse'), may hold values from -100 to 100
- taps: float32 [128], replicated, may hold values from -0.5 to 0.5
- taper: float32 [64], P('pulse'), may hold values from 0.5 to 1.5
Outputs:
- whitened: float32 [8192, 2048], P('range', 'pulse')
The draws below stay inside these ranges and needn't reach their ends.
All inputs are finite; a program needn't handle non-finite values.
Results may differ from the reference program's by a relative error of at most 0.0003.
Values sent between devices are 32-bit elements; how exact they have to be, the bound alone decides.
A program may use at most 64 MiB of HBM per device.

```python
import math
import jax
import jax.numpy as jnp
from jax import lax

RG_DEV = 1024
BINS = 16
CH = 16
TAPS = 128
GATES = 8192
PULSES = 64
N_PULSE = 4


def draw_samples(key, part):
    row_key, chan_key, base_key = jax.random.split(key, 3)
    gate_block = max(RG_DEV // 8, 1)
    total_columns = PULSES * 2 * CH
    gate_scale = jnp.exp(jax.random.uniform(row_key, (GATES // gate_block,), jnp.float32, 0.0, math.log(10.0)))
    gate_scale = jnp.repeat(gate_scale, gate_block)
    chan_scale = jnp.exp(jax.random.uniform(chan_key, (CH,), jnp.float32, 0.0, math.log(10.0)))
    column_scale = jnp.tile(jnp.repeat(chan_scale, 2), PULSES)
    noise = jax.random.truncated_normal(base_key, -4.0, 4.0, (GATES, total_columns), jnp.float32)
    return noise * gate_scale[:, None] * column_scale[None, :] / 10.0


def bell_draw(rng, extent, spread, reach, held_as=jnp.bfloat16):
    array = spread * jax.random.normal(rng, extent, jnp.float32)
    return jnp.clip(array, min=-reach, max=reach).astype(held_as)


def setup_inputs(seed: int = 0) -> dict:
    streams_of = jax.random.split(jax.random.key(seed), 4)
    return {
        "samples": draw_samples(jax.random.fold_in(streams_of[3], 71), 0),
        "taps": bell_draw(streams_of[1], (TAPS,), TAPS ** -0.5, 0.5, jnp.float32),
        "taper": jnp.clip(1.0 + 0.1 * jax.random.normal(streams_of[2], (PULSES,), jnp.float32), 0.5, 1.5),
    }


LOADING = 0.05

def toeplitz(taps, tile_rows):
    tap_count = taps.shape[0]
    padded_taps = jnp.concatenate([taps, jnp.zeros((tile_rows,), taps.dtype)])
    repeated = jnp.tile(padded_taps, tile_rows)[:tile_rows * (tap_count + tile_rows - 1)]
    return repeated.reshape(tile_rows, tap_count + tile_rows - 1)

def doppler_matrix(pulses):
    position = jnp.arange(pulses, dtype=jnp.int32)
    phase_index = position[:, None] * position[None, :] % pulses
    angles = phase_index.astype(jnp.float32) * (2.0 * math.pi / pulses)
    amplitude = 1.0 / math.sqrt(pulses)
    cosine = jnp.cos(angles) * amplitude
    sine_part = jnp.sin(angles) * amplitude
    real_in = jnp.stack([cosine, -sine_part], axis=1)
    imag_in = jnp.stack([sine_part, cosine], axis=1)
    return jnp.stack([real_in, imag_in], axis=1)

def reference(samples, taps, taper):
    tap_count = taps.shape[0]
    half_taps = tap_count // 2
    tile_rows = min(128, RG_DEV)
    padded = jnp.pad(samples, ((half_taps, half_taps), (0, 0)))
    matrix = toeplitz(taps, tile_rows)

    def compress_block(first_row):
        window = lax.dynamic_slice_in_dim(padded, first_row, tile_rows + tap_count - 1, 0)
        return jnp.dot(matrix.astype(jnp.float32), window.astype(jnp.float32), precision=lax.Precision.HIGHEST, preferred_element_type=jnp.float32)
    starts = jnp.arange(GATES // tile_rows, dtype=jnp.int32) * tile_rows
    compressed = lax.map(compress_block, starts).reshape(GATES, PULSES * 2 * CH)
    tapered = compressed * jnp.repeat(taper, 2 * CH)[None, :]
    arranged = tapered.reshape(GATES, PULSES, CH, 2)
    doppler = jnp.einsum('rpca,pabk->rkcb', arranged, doppler_matrix(PULSES), precision=lax.Precision.HIGHEST)
    doppler = doppler.reshape(GATES, N_PULSE, 2 * BINS * CH)
    identity = jnp.eye(2 * BINS * CH, dtype=jnp.float32)

    def whiten(position):
        snapshot = lax.dynamic_index_in_dim(doppler, position, 1, keepdims=False)
        covariance = jnp.dot(snapshot.T.astype(jnp.float32), snapshot.astype(jnp.float32), precision=lax.Precision.HIGHEST, preferred_element_type=jnp.float32) / GATES + LOADING * identity
        factor = jnp.linalg.cholesky(covariance)
        return lax.linalg.triangular_solve(factor, snapshot, left_side=False, lower=True, transpose_a=True)
    whitened = lax.map(whiten, jnp.arange(N_PULSE, dtype=jnp.int32))
    return jnp.transpose(whitened, (1, 0, 2)).reshape(GATES, PULSES * 2 * CH)
```

```python
import functools
import math

import jax
import jax.numpy as jnp
from jax import lax
from jax.experimental import pallas as pl
from jax.experimental.pallas import tpu as pltpu
from jax.sharding import PartitionSpec as P

LOADING = 0.05


def padded_2(block, sides, width):
    for axis, dim in sides:
        count = lax.axis_size(axis)
        forward = [(i, i + 1) for i in range(count - 1)]
        backward = [(target, source) for source, target in forward]
        low = lax.ppermute(
            lax.slice_in_dim(block, block.shape[dim] - width, None, axis=dim), axis, forward
        )
        high = lax.ppermute(lax.slice_in_dim(block, 0, width, axis=dim), axis, backward)
        block = jnp.concatenate([low, block, high], axis=dim)
    return block


def toeplitz(taps, tile_rows):
    tap_count = taps.shape[0]
    padded_taps = jnp.concatenate([taps, jnp.zeros((tile_rows,), taps.dtype)])
    repeated = jnp.tile(padded_taps, tile_rows)[: tile_rows * (tap_count + tile_rows - 1)]
    return repeated.reshape(tile_rows, tap_count + tile_rows - 1)


def doppler_matrix(pulses):
    position = jnp.arange(pulses, dtype=jnp.int32)
    phase_index = position[:, None] * position[None, :] % pulses
    angles = phase_index.astype(jnp.float32) * (2.0 * math.pi / pulses)
    amplitude = 1.0 / math.sqrt(pulses)
    cosine = jnp.cos(angles) * amplitude
    sine_part = jnp.sin(angles) * amplitude
    real_in = jnp.stack([cosine, -sine_part], axis=1)
    imag_in = jnp.stack([sine_part, cosine], axis=1)
    return jnp.stack([real_in, imag_in], axis=1)


def transform(received, doppler_table, pulses, group_width):
    part_rows = received.shape[0]
    arranged = received.reshape(part_rows, pulses, group_width // 2, 2)
    spectrum = jnp.einsum(
        "rpca,pabk->rkcb", arranged, doppler_table, precision=lax.Precision.HIGHEST
    )
    return spectrum.reshape(part_rows, pulses, group_width)


BLOCK = 128
PANEL = 16
HIGHEST = lax.Precision.HIGHEST


def split3(x):
    high = x.astype(jnp.bfloat16)
    rest = x - high.astype(jnp.float32)
    middle = rest.astype(jnp.bfloat16)
    low = (rest - middle.astype(jnp.float32)).astype(jnp.bfloat16)
    return high, middle, low


def eliminate_panel(work_ref, first, block):
    last = first + PANEL
    tile = work_ref[first:last, :]
    width = tile.shape[1]
    row = lax.broadcasted_iota(jnp.int32, (PANEL, block), 0)
    columns = [
        jnp.broadcast_to(tile[:, first + c : first + c + 1], (PANEL, block)) for c in range(PANEL)
    ]
    left, right = tile[:, :block], tile[:, block:]
    for r in range(PANEL):
        inverse = lax.rsqrt(columns[r][r : r + 1, :])
        below = jnp.where(row > r, columns[r] * inverse, 0.0)
        for c in range(r + 1, PANEL):
            columns[c] = columns[c] - below * (columns[c][r : r + 1, :] * inverse)
        left_row = left[r : r + 1, :] * inverse
        right_row = right[r : r + 1, :] * inverse
        left = jnp.where(row == r, left_row, left - below * left_row)
        right = jnp.where(row == r, right_row, right - below * right_row)
    tile = jnp.concatenate([left, right], axis=1)
    work_ref[first:last, :] = tile
    if last < block:
        high, middle, low = split3(tile)
        lhs = jnp.concatenate([high, high, middle, middle, high, low], axis=0)[:, :block]
        rhs = jnp.concatenate([high, middle, high, middle, low, high], axis=0)
        update = lax.dot_general(
            lhs, rhs, (((0,), (0,)), ((), ())), preferred_element_type=jnp.float32
        )
        work_ref[last:, :] = work_ref[last:, :] - update[last:, :]


def whiten_kernel(total_gates, gram_ref, snapshot_ref, out_ref, cov_ref, work_ref):
    size = gram_ref.shape[0]
    block = min(BLOCK, size)
    rows = lax.broadcasted_iota(jnp.int32, (size, size), 0)
    cols = lax.broadcasted_iota(jnp.int32, (size, size), 1)
    cov_ref[...] = gram_ref[...] * (1.0 / total_gates) + jnp.where(rows == cols, LOADING, 0.0)
    out_ref[...] = snapshot_ref[...]
    transposed = (((1,), (1,)), ((), ()))

    def step(index, carry):
        start = pl.multiple_of(index * block, block)
        here = pl.ds(start, block)
        r = lax.broadcasted_iota(jnp.int32, (block, block), 0)
        c = lax.broadcasted_iota(jnp.int32, (block, block), 1)
        work_ref[:, :block] = cov_ref[here, here]
        work_ref[:, block:] = jnp.where(r == c, 1.0, 0.0)
        for first in range(0, block, PANEL):
            eliminate_panel(work_ref, first, block)
        inverse = work_ref[:, block:]
        panel = lax.dot_general(
            cov_ref[:, here], inverse, transposed, precision=HIGHEST,
            preferred_element_type=jnp.float32,
        )
        below = lax.broadcasted_iota(jnp.int32, (size, block), 0) >= start + block
        panel = jnp.where(below, panel, 0.0)
        cov_ref[...] = cov_ref[...] - lax.dot_general(
            panel, panel, transposed, precision=HIGHEST, preferred_element_type=jnp.float32
        )
        solved = lax.dot_general(
            out_ref[:, here], inverse, transposed, precision=HIGHEST,
            preferred_element_type=jnp.float32,
        )
        out_ref[...] = out_ref[...] - lax.dot_general(
            solved, panel, transposed, precision=HIGHEST, preferred_element_type=jnp.float32
        )
        out_ref[:, here] = solved
        return carry

    lax.fori_loop(0, size // block, step, 0)


def whiten(gram, snapshot, total_gates):
    size = gram.shape[0]
    block = min(BLOCK, size)
    return pl.pallas_call(
        functools.partial(whiten_kernel, total_gates),
        out_shape=jax.ShapeDtypeStruct(snapshot.shape, jnp.float32),
        in_specs=[pl.BlockSpec(memory_space=pltpu.VMEM)] * 2,
        out_specs=pl.BlockSpec(memory_space=pltpu.VMEM),
        scratch_shapes=[
            pltpu.VMEM((size, size), jnp.float32),
            pltpu.VMEM((block, 2 * block), jnp.float32),
        ],
        compiler_params=pltpu.CompilerParams(vmem_limit_bytes=32 << 20),
        name="whiten",
    )(gram, snapshot)


def local(samples, taps, taper):
    gate_rows, columns = samples.shape
    tap_count = taps.shape[0]
    half_taps = tap_count // 2
    bin_count = taper.shape[0]
    pulse_devices = lax.axis_size("pulse")
    range_devices = lax.axis_size("range")
    pulses = bin_count * pulse_devices
    channels = columns // (2 * bin_count)
    padded = padded_2(samples, (("range", 0),), half_taps)
    tile_rows = min(128, gate_rows)
    matrix = toeplitz(taps, tile_rows)

    band = jnp.concatenate([matrix, jnp.zeros((tile_rows, 1), matrix.dtype)], axis=1)
    tiles = padded.reshape(-1, tile_rows, columns)
    span = gate_rows // tile_rows
    compressed = 0.0
    for part in range(band.shape[1] // tile_rows):
        compressed = compressed + jnp.einsum(
            "ab,ibj->iaj",
            band[:, part * tile_rows : (part + 1) * tile_rows],
            tiles[part : part + span],
            precision=HIGHEST,
        )
    compressed = compressed.reshape(gate_rows, columns)
    tapered = compressed * jnp.repeat(taper, 2 * channels)[None, :]
    doppler_table = doppler_matrix(pulses)
    gathered = lax.all_to_all(tapered, "pulse", split_axis=0, concat_axis=1, tiled=True)
    spectrum = transform(gathered, doppler_table, pulses, 2 * channels).reshape(
        gathered.shape[0], pulses * 2 * channels
    )
    doppler = lax.all_to_all(spectrum, "pulse", split_axis=1, concat_axis=0, tiled=True)
    total_gates = gate_rows * range_devices
    local_gram = lax.dot_general(
        doppler, doppler, (((0,), (0,)), ((), ())), precision=lax.Precision.HIGHEST
    )
    summed = lax.psum(local_gram, "range")
    return whiten(summed, doppler, total_gates)


def solution(mesh):
    placed = (P("range", "pulse"), P(), P("pulse"))
    return jax.shard_map(
        local, mesh=mesh, in_specs=placed, out_specs=P("range", "pulse"), check_vma=False
    )
```

```python
import functools
import math

import jax
import jax.numpy as jnp
from jax import lax
from jax.experimental import pallas as pl
from jax.experimental.pallas import tpu as pltpu
from jax.sharding import PartitionSpec as P

LOADING = 0.05


def padded_2(block, sides, width):
    for axis, dim in sides:
        count = lax.axis_size(axis)
        forward = [(i, i + 1) for i in range(count - 1)]
        backward = [(target, source) for source, target in forward]
        low = lax.ppermute(
            lax.slice_in_dim(block, block.shape[dim] - width, None, axis=dim), axis, forward
        )
        high = lax.ppermute(lax.slice_in_dim(block, 0, width, axis=dim), axis, backward)
        block = jnp.concatenate([low, block, high], axis=dim)
    return block


def toeplitz(taps, tile_rows):
    tap_count = taps.shape[0]
    padded_taps = jnp.concatenate([taps, jnp.zeros((tile_rows,), taps.dtype)])
    repeated = jnp.tile(padded_taps, tile_rows)[: tile_rows * (tap_count + tile_rows - 1)]
    return repeated.reshape(tile_rows, tap_count + tile_rows - 1)


def doppler_matrix(pulses):
    position = jnp.arange(pulses, dtype=jnp.int32)
    phase_index = position[:, None] * position[None, :] % pulses
    angles = phase_index.astype(jnp.float32) * (2.0 * math.pi / pulses)
    amplitude = 1.0 / math.sqrt(pulses)
    cosine = jnp.cos(angles) * amplitude
    sine_part = jnp.sin(angles) * amplitude
    real_in = jnp.stack([cosine, -sine_part], axis=1)
    imag_in = jnp.stack([sine_part, cosine], axis=1)
    return jnp.stack([real_in, imag_in], axis=1)


def transform(received, doppler_table, pulses, group_width):
    part_rows = received.shape[0]
    arranged = received.reshape(part_rows, pulses, group_width // 2, 2)
    spectrum = jnp.einsum(
        "rpca,pabk->rkcb", arranged, doppler_table, precision=lax.Precision.HIGHEST
    )
    return spectrum.reshape(part_rows, pulses, group_width)


BLOCK = 128
PANEL = 16
HIGHEST = lax.Precision.HIGHEST


def split3(x):
    high = x.astype(jnp.bfloat16)
    rest = x - high.astype(jnp.float32)
    middle = rest.astype(jnp.bfloat16)
    low = (rest - middle.astype(jnp.float32)).astype(jnp.bfloat16)
    return high, middle, low


def eliminate_panel(work_ref, first, block):
    last = first + PANEL
    tile = work_ref[first:last, :]
    width = tile.shape[1]
    row = lax.broadcasted_iota(jnp.int32, (PANEL, block), 0)
    columns = [
        jnp.broadcast_to(tile[:, first + c : first + c + 1], (PANEL, block)) for c in range(PANEL)
    ]
    left, right = tile[:, :block], tile[:, block:]
    for r in range(PANEL):
        inverse = lax.rsqrt(columns[r][r : r + 1, :])
        below = jnp.where(row > r, columns[r] * inverse, 0.0)
        for c in range(r + 1, PANEL):
            columns[c] = columns[c] - below * (columns[c][r : r + 1, :] * inverse)
        left_row = left[r : r + 1, :] * inverse
        right_row = right[r : r + 1, :] * inverse
        left = jnp.where(row == r, left_row, left - below * left_row)
        right = jnp.where(row == r, right_row, right - below * right_row)
    tile = jnp.concatenate([left, right], axis=1)
    work_ref[first:last, :] = tile
    if last < block:
        high, middle, low = split3(tile)
        lhs = jnp.concatenate([high, high, middle, middle, high, low], axis=0)[:, :block]
        rhs = jnp.concatenate([high, middle, high, middle, low, high], axis=0)
        update = lax.dot_general(
            lhs, rhs, (((0,), (0,)), ((), ())), preferred_element_type=jnp.float32
        )
        work_ref[last:, :] = work_ref[last:, :] - update[last:, :]


def lower_blocks(size, block):
    pairs = [(b, c) for b in range(size // block) for c in range(b + 1)]
    return [(b * block, c * block, n * block) for n, (b, c) in enumerate(pairs)]


def sum_over_range(part_ref, pair_ref, half_ref, inbox_ref, total_ref, sems):
    pair_send, pair_recv, out_send, out_recv, back_send, back_recv, side_send, side_recv = sems
    me, count = lax.axis_index("range"), lax.axis_size("range")
    groups = count // 2
    side, group = lax.rem(me, 2), me // 2
    sibling = me + 1 - 2 * side
    half, chunk = half_ref.shape[0], half_ref.shape[0] // groups

    def send(src, dst, send_sem, recv_sem, target):
        copy = pltpu.make_async_remote_copy(
            src_ref=src, dst_ref=dst, send_sem=send_sem, recv_sem=recv_sem,
            device_id={"range": target}, device_id_type=pl.DeviceIdType.MESH,
        )
        copy.start()
        return copy

    def peer(shift):
        return 2 * lax.rem(group + shift, groups) + side

    def rows(whose, of_group):
        return pl.ds(pl.multiple_of(whose * half + of_group * chunk, 8), chunk)

    theirs = pl.ds(pl.multiple_of((1 - side) * half, 8), half)
    mine = pl.ds(pl.multiple_of(side * half, 8), half)
    first = send(part_ref.at[theirs], pair_ref, pair_send, pair_recv, sibling)
    first.wait_recv()
    half_ref[...] = part_ref[mine] + pair_ref[...]
    outs = []
    for shift in range(1, groups):
        to = lax.rem(group + shift, groups)
        outs.append(
            send(
                half_ref.at[rows(0, to)], inbox_ref.at[shift - 1],
                out_send.at[shift - 1], out_recv.at[shift - 1], peer(shift),
            )
        )
    own = half_ref[rows(0, group)]
    for shift in range(1, groups):
        outs[shift - 1].wait_recv()
        own = own + inbox_ref[shift - 1]
    total_ref[rows(side, group)] = own
    source = total_ref.at[rows(side, group)]
    backs = [
        send(source, source, back_send.at[s - 1], back_recv.at[s - 1], peer(s))
        for s in range(1, groups)
    ]
    sides = [send(source, source, side_send.at[0], side_recv.at[0], sibling)]
    for shift in range(1, groups):
        backs[shift - 1].wait_recv()
        landed = total_ref.at[rows(side, lax.rem(group + groups - shift, groups))]
        sides.append(send(landed, landed, side_send.at[shift], side_recv.at[shift], sibling))
    for copy in sides:
        copy.wait_recv()
    for copy in [first] + outs + backs + sides:
        copy.wait_send()


def greet(axis_targets):
    barrier = pltpu.get_barrier_semaphore()
    for axis, target in axis_targets:
        pl.semaphore_signal(
            barrier, inc=1, device_id={axis: target}, device_id_type=pl.DeviceIdType.MESH
        )
    pl.semaphore_wait(barrier, len(axis_targets))


def range_partners():
    me, count = lax.axis_index("range"), lax.axis_size("range")
    groups, side, group = count // 2, lax.rem(me, 2), me // 2
    found = [("range", me + 1 - 2 * side)]
    for shift in range(1, groups):
        found.append(("range", 2 * lax.rem(group + shift, groups) + side))
    return found


def factor_and_solve(total_gates, total_ref, out_ref, cov_ref, work_ref):
    size = cov_ref.shape[0]
    block = work_ref.shape[0]
    r = lax.broadcasted_iota(jnp.int32, (block, block), 0)
    c = lax.broadcasted_iota(jnp.int32, (block, block), 1)
    cov_ref[...] = jnp.zeros_like(cov_ref)
    for row, col, at in lower_blocks(size, block):
        value = total_ref[at : at + block, :] * (1.0 / total_gates)
        if row == col:
            value = value + jnp.where(r == c, LOADING, 0.0)
        cov_ref[row : row + block, col : col + block] = value
    transposed = (((1,), (1,)), ((), ()))

    def dot(x, y):
        return lax.dot_general(
            x, y, transposed, precision=HIGHEST, preferred_element_type=jnp.float32
        )

    for start in range(0, size, block):
        end = start + block
        work_ref[:, :block] = cov_ref[start:end, start:end]
        work_ref[:, block:] = jnp.where(r == c, 1.0, 0.0)
        for first in range(0, block, PANEL):
            eliminate_panel(work_ref, first, block)
        inverse = work_ref[:, block:]
        solved = dot(out_ref[:, start:end], inverse)
        out_ref[:, start:end] = solved
        if end < size:
            panel = dot(cov_ref[end:, start:end], inverse)
            cov_ref[end:, end:] = cov_ref[end:, end:] - dot(panel, panel)
            out_ref[:, end:] = out_ref[:, end:] - dot(solved, panel)


def whiten_kernel(
    total_gates, snapshot_ref, out_ref, part_ref, pair_ref, half_ref, inbox_ref, total_ref,
    cov_ref, work_ref, *sems
):
    size = snapshot_ref.shape[1]
    block = work_ref.shape[0]
    for row in range(0, size, block):
        gram = lax.dot_general(
            snapshot_ref[:, row : row + block], snapshot_ref[:, : row + block],
            (((0,), (0,)), ((), ())), precision=HIGHEST, preferred_element_type=jnp.float32,
        )
        for b_row, b_col, at in lower_blocks(size, block):
            if b_row == row:
                part_ref[at : at + block, :] = gram[:, b_col : b_col + block]
    greet(range_partners())
    sum_over_range(part_ref, pair_ref, half_ref, inbox_ref, total_ref, sems)
    out_ref[...] = snapshot_ref[...]
    factor_and_solve(total_gates, total_ref, out_ref, cov_ref, work_ref)


def whiten_scratch(size, block, groups):
    packed = len(lower_blocks(size, block)) * block
    half = packed // 2
    assert half % (8 * groups) == 0
    dma = pltpu.SemaphoreType.DMA
    others = max(groups - 1, 1)
    return [
        pltpu.VMEM((packed, block), jnp.float32),
        pltpu.VMEM((half, block), jnp.float32),
        pltpu.VMEM((half, block), jnp.float32),
        pltpu.VMEM((others, half // groups, block), jnp.float32),
        pltpu.VMEM((packed, block), jnp.float32),
        pltpu.VMEM((size, size), jnp.float32),
        pltpu.VMEM((block, 2 * block), jnp.float32),
        dma, dma, dma((others,)), dma((others,)), dma((others,)), dma((others,)),
        dma((groups,)), dma((groups,)),
    ]


def whiten(snapshot, total_gates):
    size = snapshot.shape[1]
    block = min(BLOCK, size)
    return pl.pallas_call(
        functools.partial(whiten_kernel, total_gates),
        out_shape=jax.ShapeDtypeStruct(snapshot.shape, jnp.float32),
        in_specs=[pl.BlockSpec(memory_space=pltpu.VMEM)],
        out_specs=pl.BlockSpec(memory_space=pltpu.VMEM),
        scratch_shapes=whiten_scratch(size, block, lax.axis_size("range") // 2),
        compiler_params=pltpu.CompilerParams(
            vmem_limit_bytes=32 << 20, collective_id=1, has_side_effects=True
        ),
        name="whiten",
    )(snapshot)


def local(samples, taps, taper):
    gate_rows, columns = samples.shape
    tap_count = taps.shape[0]
    half_taps = tap_count // 2
    bin_count = taper.shape[0]
    pulse_devices = lax.axis_size("pulse")
    range_devices = lax.axis_size("range")
    pulses = bin_count * pulse_devices
    channels = columns // (2 * bin_count)
    padded = padded_2(samples, (("range", 0),), half_taps)
    tile_rows = min(128, gate_rows)
    matrix = toeplitz(taps, tile_rows)

    band = jnp.concatenate([matrix, jnp.zeros((tile_rows, 1), matrix.dtype)], axis=1)
    tiles = padded.reshape(-1, tile_rows, columns)
    span = gate_rows // tile_rows
    compressed = 0.0
    for part in range(band.shape[1] // tile_rows):
        compressed = compressed + jnp.einsum(
            "ab,ibj->iaj",
            band[:, part * tile_rows : (part + 1) * tile_rows],
            tiles[part : part + span],
            precision=HIGHEST,
        )
    compressed = compressed.reshape(gate_rows, columns)
    tapered = compressed * jnp.repeat(taper, 2 * channels)[None, :]
    doppler_table = doppler_matrix(pulses)
    gathered = lax.all_to_all(tapered, "pulse", split_axis=0, concat_axis=1, tiled=True)
    spectrum = transform(gathered, doppler_table, pulses, 2 * channels).reshape(
        gathered.shape[0], pulses * 2 * channels
    )
    doppler = lax.all_to_all(spectrum, "pulse", split_axis=1, concat_axis=0, tiled=True)
    total_gates = gate_rows * range_devices
    return whiten(doppler, total_gates)


def solution(mesh):
    placed = (P("range", "pulse"), P(), P("pulse"))
    return jax.shard_map(
        local, mesh=mesh, in_specs=placed, out_specs=P("range", "pulse"), check_vma=False
    )
```

```python
import functools
import math

import jax
import jax.numpy as jnp
import numpy as np
from jax import lax
from jax.experimental import pallas as pl
from jax.experimental.pallas import tpu as pltpu
from jax.sharding import PartitionSpec as P

LOADING = 0.05


BLOCK = 128
PANEL = 16
LANES = 128
CHUNKS = 4
HIGHEST = lax.Precision.HIGHEST


def split3(x):
    high = x.astype(jnp.bfloat16)
    rest = x - high.astype(jnp.float32)
    middle = rest.astype(jnp.bfloat16)
    low = (rest - middle.astype(jnp.float32)).astype(jnp.bfloat16)
    return high, middle, low


def eliminate_panel(work_ref, first, block):
    last = first + PANEL
    tile = work_ref[first:last, :]
    width = tile.shape[1]
    row = lax.broadcasted_iota(jnp.int32, (PANEL, block), 0)
    columns = [
        jnp.broadcast_to(tile[:, first + c : first + c + 1], (PANEL, block)) for c in range(PANEL)
    ]
    left, right = tile[:, :block], tile[:, block:]
    for r in range(PANEL):
        inverse = lax.rsqrt(columns[r][r : r + 1, :])
        below = jnp.where(row > r, columns[r] * inverse, 0.0)
        for c in range(r + 1, PANEL):
            columns[c] = columns[c] - below * (columns[c][r : r + 1, :] * inverse)
        left_row = left[r : r + 1, :] * inverse
        right_row = right[r : r + 1, :] * inverse
        left = jnp.where(row == r, left_row, left - below * left_row)
        right = jnp.where(row == r, right_row, right - below * right_row)
    tile = jnp.concatenate([left, right], axis=1)
    work_ref[first:last, :] = tile
    if last < block:
        high, middle, low = split3(tile)
        lhs = jnp.concatenate([high, high, middle, middle, high, low], axis=0)[:, :block]
        rhs = jnp.concatenate([high, middle, high, middle, low, high], axis=0)
        update = lax.dot_general(
            lhs, rhs, (((0,), (0,)), ((), ())), preferred_element_type=jnp.float32
        )
        work_ref[last:, :] = work_ref[last:, :] - update[last:, :]


def lower_blocks(size, block):
    pairs = [(b, c) for b in range(size // block) for c in range(b + 1)]
    return [(b * block, c * block, n * block) for n, (b, c) in enumerate(pairs)]


def sum_over_range(part_ref, pair_ref, half_ref, inbox_ref, total_ref, sems):
    pair_send, pair_recv, out_send, out_recv, back_send, back_recv, side_send, side_recv = sems
    me, count = lax.axis_index("range"), lax.axis_size("range")
    groups = count // 2
    side, group = lax.rem(me, 2), me // 2
    sibling = me + 1 - 2 * side
    half, chunk = half_ref.shape[0], half_ref.shape[0] // groups

    def send(src, dst, send_sem, recv_sem, target):
        copy = pltpu.make_async_remote_copy(
            src_ref=src, dst_ref=dst, send_sem=send_sem, recv_sem=recv_sem,
            device_id={"range": target}, device_id_type=pl.DeviceIdType.MESH,
        )
        copy.start()
        return copy

    def peer(shift):
        return 2 * lax.rem(group + shift, groups) + side

    def rows(whose, of_group):
        return pl.ds(pl.multiple_of(whose * half + of_group * chunk, 8), chunk)

    theirs = pl.ds(pl.multiple_of((1 - side) * half, 8), half)
    mine = pl.ds(pl.multiple_of(side * half, 8), half)
    first = send(part_ref.at[theirs], pair_ref, pair_send, pair_recv, sibling)
    first.wait_recv()
    half_ref[...] = part_ref[mine] + pair_ref[...]
    outs = []
    for shift in range(1, groups):
        to = lax.rem(group + shift, groups)
        outs.append(
            send(
                half_ref.at[rows(0, to)], inbox_ref.at[shift - 1],
                out_send.at[shift - 1], out_recv.at[shift - 1], peer(shift),
            )
        )
    own = half_ref[rows(0, group)]
    for shift in range(1, groups):
        outs[shift - 1].wait_recv()
        own = own + inbox_ref[shift - 1]
    total_ref[rows(side, group)] = own
    source = total_ref.at[rows(side, group)]
    backs = [
        send(source, source, back_send.at[s - 1], back_recv.at[s - 1], peer(s))
        for s in range(1, groups)
    ]
    sides = [send(source, source, side_send.at[0], side_recv.at[0], sibling)]
    for shift in range(1, groups):
        backs[shift - 1].wait_recv()
        landed = total_ref.at[rows(side, lax.rem(group + groups - shift, groups))]
        sides.append(send(landed, landed, side_send.at[shift], side_recv.at[shift], sibling))
    for copy in sides:
        copy.wait_recv()
    for copy in [first] + outs + backs + sides:
        copy.wait_send()


def greet(axis_targets):
    barrier = pltpu.get_barrier_semaphore()
    for axis, target in axis_targets:
        pl.semaphore_signal(
            barrier, inc=1, device_id={axis: target}, device_id_type=pl.DeviceIdType.MESH
        )
    pl.semaphore_wait(barrier, len(axis_targets))


def range_partners():
    me, count = lax.axis_index("range"), lax.axis_size("range")
    groups, side, group = count // 2, lax.rem(me, 2), me // 2
    found = [("range", me + 1 - 2 * side)]
    for shift in range(1, groups):
        found.append(("range", 2 * lax.rem(group + shift, groups) + side))
    return found


def factor_and_solve(total_gates, total_ref, out_ref, cov_ref, work_ref):
    size = cov_ref.shape[0]
    block = work_ref.shape[0]
    r = lax.broadcasted_iota(jnp.int32, (block, block), 0)
    c = lax.broadcasted_iota(jnp.int32, (block, block), 1)
    cov_ref[...] = jnp.zeros_like(cov_ref)
    for row, col, at in lower_blocks(size, block):
        value = total_ref[at : at + block, :] * (1.0 / total_gates)
        if row == col:
            value = value + jnp.where(r == c, LOADING, 0.0)
        cov_ref[row : row + block, col : col + block] = value
    transposed = (((1,), (1,)), ((), ()))

    def dot(x, y):
        return lax.dot_general(
            x, y, transposed, precision=HIGHEST, preferred_element_type=jnp.float32
        )

    for start in range(0, size, block):
        end = start + block
        work_ref[:, :block] = cov_ref[start:end, start:end]
        work_ref[:, block:] = jnp.where(r == c, 1.0, 0.0)
        for first in range(0, block, PANEL):
            eliminate_panel(work_ref, first, block)
        inverse = work_ref[:, block:]
        solved = dot(out_ref[:, start:end], inverse)
        out_ref[:, start:end] = solved
        if end < size:
            panel = dot(cov_ref[end:, start:end], inverse)
            cov_ref[end:, end:] = cov_ref[end:, end:] - dot(panel, panel)
            out_ref[:, end:] = out_ref[:, end:] - dot(solved, panel)


def quarter_turn(x):
    lane = lax.broadcasted_iota(jnp.int32, x.shape, 1)
    width = x.shape[1]
    return jnp.where(
        lane % 2 == 0, pltpu.roll(x, width - 1, axis=1), -pltpu.roll(x, 1, axis=1)
    )


def doppler_constants(pulses, devices, group):
    bins = pulses // devices
    lane = np.arange(bins * group)
    turn = (lane // group)[None, :] * np.arange(devices)[:, None] % pulses
    angle = turn * (2.0 * math.pi / pulses)
    first = np.arange(bins)
    phase = (first[:, None] * first[None, :] % bins) * (2.0 * math.pi / bins)
    cosine, sine = np.cos(phase), np.sin(phase)
    pair = np.stack(
        [np.stack([cosine, -sine], axis=-1), np.stack([sine, cosine], axis=-1)], axis=1
    ) / math.sqrt(pulses)
    table = np.einsum("paqb,cd->pcaqdb", pair, np.eye(group // 2))
    table = table.reshape(bins * group, bins * group)
    return tuple(np.asarray(v, np.float32) for v in (np.cos(angle), np.sin(angle), table))


def transform_chunk(rows, group, gathered_ref, cos_ref, sin_ref, table_ref, stage_ref, spread_ref):
    devices, _, width = gathered_ref.shape
    count = rows.size
    bins = width // group
    for at in range(0, width, LANES):
        lanes = slice(at, at + LANES)
        parts = [gathered_ref[z, rows, lanes] for z in range(devices)]
        turned = [quarter_turn(x) for x in parts]
        for k in range(devices):
            total = None
            for z in range(devices):
                step = z * k % devices
                for weight, term in (
                    (math.cos(2.0 * math.pi * step / devices), parts[z]),
                    (math.sin(2.0 * math.pi * step / devices), turned[z]),
                ):
                    if abs(weight) < 1e-9:
                        continue
                    sign = 1.0 if weight > 0 else -1.0
                    if abs(abs(weight) - 1.0) > 1e-9:
                        term, sign = term * weight, 1.0
                    if total is None:
                        total = term if sign > 0 else -term
                    else:
                        total = total + term if sign > 0 else total - term
            total = total * cos_ref[k : k + 1, lanes] + quarter_turn(total) * sin_ref[
                k : k + 1, lanes
            ]
            stage_ref[k * count : (k + 1) * count, lanes] = total
    mixed = jnp.dot(
        stage_ref[...], table_ref[...], precision=HIGHEST, preferred_element_type=jnp.float32
    )
    place = lax.broadcasted_iota(jnp.int32, (count, LANES), 1) // group
    for target in range(devices):
        for at in range(0, width, LANES):
            out = None
            for n in range(LANES // group):
                k = target * bins + at // group + n
                low, high = k % devices, k // devices
                source = high * group
                block = source // LANES * LANES
                piece = mixed[low * count : (low + 1) * count, block : block + LANES]
                shift = (n * group - source) % LANES
                if shift:
                    piece = pltpu.roll(piece, shift, axis=1)
                out = piece if out is None else jnp.where(place == n, piece, out)
            spread_ref[target, rows, at : at + LANES] = out


def exchange(
    samples_ref, taps_ref, taper_ref, cos_ref, sin_ref, table_ref, snapshot_ref,
    low_ref, high_ref, padded_ref, outgoing_ref, gathered_ref, stage_ref, spread_ref, group, sems
):
    halo_send, halo_recv, in_send, in_recv, back_send, back_recv = sems
    gates, width = samples_ref.shape
    devices, share, _ = gathered_ref.shape
    half = low_ref.shape[0]
    count = share // CHUNKS
    z = lax.axis_index("pulse")
    me, ranges = lax.axis_index("range"), lax.axis_size("range")

    def send(src, dst, send_sem, recv_sem, axis, target):
        copy = pltpu.make_async_remote_copy(
            src_ref=src, dst_ref=dst, send_sem=send_sem, recv_sem=recv_sem,
            device_id={axis: target}, device_id_type=pl.DeviceIdType.MESH,
        )
        copy.start()
        return copy

    halos = [
        send(
            samples_ref.at[gates - half :], low_ref, halo_send.at[0], halo_recv.at[0],
            "range", lax.rem(me + 1, ranges),
        ),
        send(
            samples_ref.at[:half], high_ref, halo_send.at[1], halo_recv.at[1],
            "range", lax.rem(me + ranges - 1, ranges),
        ),
    ]
    padded_ref[half : half + gates, :] = samples_ref[...]
    taps = jnp.broadcast_to(taps_ref[...], (count, taps_ref.shape[1]))
    span = count + 2 * half
    band = pltpu.roll(taps, 0, axis=1, stride=1, stride_axis=0)[:, :span]
    for copy in halos:
        copy.wait_recv()
    padded_ref[:half, :] = jnp.where(me > 0, low_ref[...], 0.0)
    padded_ref[half + gates :, :] = jnp.where(me < ranges - 1, high_ref[...], 0.0)
    shifts = sorted(range(1, devices), key=lambda s: abs(2 * s - devices))
    ins = {}
    for part in range(CHUNKS):
        for shift in shifts + [0]:
            target = lax.rem(z + shift, devices)
            start = pl.multiple_of(target * share + part * count, 8)
            value = taper_ref[...] * jnp.dot(
                band, padded_ref[pl.ds(start, span), :], precision=HIGHEST,
                preferred_element_type=jnp.float32,
            )
            rows = pl.ds(part * count, count)
            if shift == 0:
                gathered_ref[z, rows, :] = value
                continue
            here = outgoing_ref.at[pl.ds(start, count)]
            here[...] = value
            ins[part, shift] = send(
                here, gathered_ref.at[z, rows], in_send.at[shift - 1, part],
                in_recv.at[shift - 1, part], "pulse", target,
            )
    backs = []
    for part in range(CHUNKS):
        rows = pl.ds(part * count, count)
        for shift in shifts:
            ins[part, shift].wait_recv()
        transform_chunk(
            rows, group, gathered_ref, cos_ref, sin_ref, table_ref, stage_ref, spread_ref
        )
        home = pl.ds(pl.multiple_of(z * share + part * count, 8), count)
        for shift in shifts:
            target = lax.rem(z + shift, devices)
            backs.append(
                send(
                    spread_ref.at[target, rows], snapshot_ref.at[home],
                    back_send.at[shift - 1, part], back_recv.at[shift - 1, part],
                    "pulse", target,
                )
            )
        snapshot_ref[home, :] = spread_ref[z, rows, :]
    for copy in backs:
        copy.wait_recv()
    for copy in halos + list(ins.values()) + backs:
        copy.wait_send()


def whole_kernel(
    total_gates, group, samples_ref, taps_ref, taper_ref, cos_ref, sin_ref, table_ref, out_ref,
    snapshot_ref, low_ref, high_ref, padded_ref, outgoing_ref, gathered_ref, stage_ref,
    spread_ref, part_ref, pair_ref, half_ref, inbox_ref, total_ref, cov_ref, work_ref, *sems
):
    z, devices = lax.axis_index("pulse"), lax.axis_size("pulse")
    me, ranges = lax.axis_index("range"), lax.axis_size("range")
    greet(
        range_partners()
        + [("range", lax.rem(me + 1, ranges)), ("range", lax.rem(me + ranges - 1, ranges))]
        + [("pulse", lax.rem(z + shift, devices)) for shift in range(1, devices)]
    )
    exchange(
        samples_ref, taps_ref, taper_ref, cos_ref, sin_ref, table_ref, snapshot_ref,
        low_ref, high_ref, padded_ref, outgoing_ref, gathered_ref, stage_ref, spread_ref, group,
        sems[:6],
    )
    size = snapshot_ref.shape[1]
    block = work_ref.shape[0]
    for row in range(0, size, block):
        gram = lax.dot_general(
            snapshot_ref[:, row : row + block], snapshot_ref[:, : row + block],
            (((0,), (0,)), ((), ())), precision=HIGHEST, preferred_element_type=jnp.float32,
        )
        for b_row, b_col, at in lower_blocks(size, block):
            if b_row == row:
                part_ref[at : at + block, :] = gram[:, b_col : b_col + block]
    sum_over_range(part_ref, pair_ref, half_ref, inbox_ref, total_ref, sems[6:])
    out_ref[...] = snapshot_ref[...]
    factor_and_solve(total_gates, total_ref, out_ref, cov_ref, work_ref)


def whiten_scratch(size, block, groups):
    packed = len(lower_blocks(size, block)) * block
    half = packed // 2
    assert half % (8 * groups) == 0
    dma = pltpu.SemaphoreType.DMA
    others = max(groups - 1, 1)
    return [
        pltpu.VMEM((packed, block), jnp.float32),
        pltpu.VMEM((half, block), jnp.float32),
        pltpu.VMEM((half, block), jnp.float32),
        pltpu.VMEM((others, half // groups, block), jnp.float32),
        pltpu.VMEM((packed, block), jnp.float32),
        pltpu.VMEM((size, size), jnp.float32),
        pltpu.VMEM((block, 2 * block), jnp.float32),
    ], [
        dma, dma, dma((others,)), dma((others,)), dma((others,)), dma((others,)),
        dma((groups,)), dma((groups,)),
    ]


def local(samples, taps, taper):
    gates, width = samples.shape
    tap_count = taps.shape[0]
    half = tap_count // 2
    bins = taper.shape[0]
    devices, ranges = lax.axis_size("pulse"), lax.axis_size("range")
    group = width // bins
    share = gates // devices
    count = share // CHUNKS
    block = min(BLOCK, width)
    cosine, sine, table = doppler_constants(bins * devices, devices, group)
    room = -(-(tap_count + count) // LANES) * LANES
    padded_taps = jnp.pad(taps, (0, room - tap_count))[None, :]
    taper_row = jnp.repeat(taper, group)[None, :]
    buffers, sems = whiten_scratch(width, block, ranges // 2)
    dma = pltpu.SemaphoreType.DMA
    own = [
        pltpu.VMEM((gates, width), jnp.float32),
        pltpu.VMEM((half, width), jnp.float32),
        pltpu.VMEM((half, width), jnp.float32),
        pltpu.VMEM((gates + 2 * half, width), jnp.float32),
        pltpu.VMEM((gates, width), jnp.float32),
        pltpu.VMEM((devices, share, width), jnp.float32),
        pltpu.VMEM((devices * count, width), jnp.float32),
        pltpu.VMEM((devices, share, width), jnp.float32),
    ]
    pulse_sems = [dma((2,)), dma((2,))] + [dma((devices - 1, CHUNKS))] * 4
    return pl.pallas_call(
        functools.partial(whole_kernel, gates * ranges, group),
        out_shape=jax.ShapeDtypeStruct(samples.shape, jnp.float32),
        in_specs=[pl.BlockSpec(memory_space=pltpu.VMEM)] * 6,
        out_specs=pl.BlockSpec(memory_space=pltpu.VMEM),
        scratch_shapes=own + buffers + pulse_sems + sems,
        compiler_params=pltpu.CompilerParams(
            vmem_limit_bytes=48 << 20, collective_id=1, has_side_effects=True
        ),
        name="whiten",
    )(samples, padded_taps, taper_row, cosine, sine, table)


def solution(mesh):
    placed = (P("range", "pulse"), P(), P("pulse"))
    return jax.shard_map(
        local, mesh=mesh, in_specs=placed, out_specs=P("range", "pulse"), check_vma=False
    )
```

```python
import functools
import math

import jax
import jax.numpy as jnp
import numpy as np
from jax import lax
from jax.experimental import pallas as pl
from jax.experimental.pallas import tpu as pltpu
from jax.sharding import PartitionSpec as P

LOADING = 0.05


BLOCK = 128
PANEL = 16
LANES = 128
CHUNKS = 4
HIGHEST = lax.Precision.HIGHEST


def split3(x):
    high = x.astype(jnp.bfloat16)
    rest = x - high.astype(jnp.float32)
    middle = rest.astype(jnp.bfloat16)
    low = (rest - middle.astype(jnp.float32)).astype(jnp.bfloat16)
    return high, middle, low


def eliminate_panel(work_ref, first, block):
    last = first + PANEL
    tile = work_ref[first:last, :]
    width = tile.shape[1]
    row = lax.broadcasted_iota(jnp.int32, (PANEL, block), 0)
    columns = [
        jnp.broadcast_to(tile[:, first + c : first + c + 1], (PANEL, block)) for c in range(PANEL)
    ]
    left, right = tile[:, :block], tile[:, block:]
    for r in range(PANEL):
        inverse = lax.rsqrt(columns[r][r : r + 1, :])
        below = jnp.where(row > r, columns[r] * inverse, 0.0)
        for c in range(r + 1, PANEL):
            columns[c] = columns[c] - below * (columns[c][r : r + 1, :] * inverse)
        left_row = left[r : r + 1, :] * inverse
        right_row = right[r : r + 1, :] * inverse
        left = jnp.where(row == r, left_row, left - below * left_row)
        right = jnp.where(row == r, right_row, right - below * right_row)
    tile = jnp.concatenate([left, right], axis=1)
    work_ref[first:last, :] = tile
    if last < block:
        high, middle, low = split3(tile)
        lhs = jnp.concatenate([high, high, middle, middle, high, low], axis=0)[:, :block]
        rhs = jnp.concatenate([high, middle, high, middle, low, high], axis=0)
        update = lax.dot_general(
            lhs, rhs, (((0,), (0,)), ((), ())), preferred_element_type=jnp.float32
        )
        work_ref[last:, :] = work_ref[last:, :] - update[last:, :]


def lower_blocks(size, block):
    pairs = [(b, c) for b in range(size // block) for c in range(b + 1)]
    return [(b * block, c * block, n * block) for n, (b, c) in enumerate(pairs)]


def sum_over_range(part_ref, pair_ref, half_ref, inbox_ref, total_ref, sems):
    pair_send, pair_recv, out_send, out_recv, back_send, back_recv, side_send, side_recv = sems
    me, count = lax.axis_index("range"), lax.axis_size("range")
    groups = count // 2
    side, group = lax.rem(me, 2), me // 2
    sibling = me + 1 - 2 * side
    half, chunk = half_ref.shape[0], half_ref.shape[0] // groups

    def send(src, dst, send_sem, recv_sem, target):
        copy = pltpu.make_async_remote_copy(
            src_ref=src, dst_ref=dst, send_sem=send_sem, recv_sem=recv_sem,
            device_id={"range": target}, device_id_type=pl.DeviceIdType.MESH,
        )
        copy.start()
        return copy

    def peer(shift):
        return 2 * lax.rem(group + shift, groups) + side

    def rows(whose, of_group):
        return pl.ds(pl.multiple_of(whose * half + of_group * chunk, 8), chunk)

    theirs = pl.ds(pl.multiple_of((1 - side) * half, 8), half)
    mine = pl.ds(pl.multiple_of(side * half, 8), half)
    first = send(part_ref.at[theirs], pair_ref, pair_send, pair_recv, sibling)
    first.wait_recv()
    half_ref[...] = part_ref[mine] + pair_ref[...]
    outs = []
    for shift in range(1, groups):
        to = lax.rem(group + shift, groups)
        outs.append(
            send(
                half_ref.at[rows(0, to)], inbox_ref.at[shift - 1],
                out_send.at[shift - 1], out_recv.at[shift - 1], peer(shift),
            )
        )
    own = half_ref[rows(0, group)]
    for shift in range(1, groups):
        outs[shift - 1].wait_recv()
        own = own + inbox_ref[shift - 1]
    total_ref[rows(side, group)] = own
    source = total_ref.at[rows(side, group)]
    backs = [
        send(source, source, back_send.at[s - 1], back_recv.at[s - 1], peer(s))
        for s in range(1, groups)
    ]
    sides = [send(source, source, side_send.at[0], side_recv.at[0], sibling)]
    for shift in range(1, groups):
        backs[shift - 1].wait_recv()
        landed = total_ref.at[rows(side, lax.rem(group + groups - shift, groups))]
        sides.append(send(landed, landed, side_send.at[shift], side_recv.at[shift], sibling))
    for copy in sides:
        copy.wait_recv()
    for copy in [first] + outs + backs + sides:
        copy.wait_send()


def greet(axis_targets):
    barrier = pltpu.get_barrier_semaphore()
    for axis, target in axis_targets:
        pl.semaphore_signal(
            barrier, inc=1, device_id={axis: target}, device_id_type=pl.DeviceIdType.MESH
        )
    pl.semaphore_wait(barrier, len(axis_targets))


def range_partners():
    me, count = lax.axis_index("range"), lax.axis_size("range")
    groups, side, group = count // 2, lax.rem(me, 2), me // 2
    found = [("range", me + 1 - 2 * side)]
    for shift in range(1, groups):
        found.append(("range", 2 * lax.rem(group + shift, groups) + side))
    return found


def factor_and_solve(
    total_gates, total_ref, data_ref, cov_ref, work_ref, inverse_ref, panel_ref, emit
):
    size = cov_ref.shape[0]
    block = work_ref.shape[0]
    r = lax.broadcasted_iota(jnp.int32, (block, block), 0)
    c = lax.broadcasted_iota(jnp.int32, (block, block), 1)
    for row, col, at in lower_blocks(size, block):
        value = total_ref[at : at + block, :] * (1.0 / total_gates)
        if row == col:
            value = value + jnp.where(r == c, LOADING, 0.0)
        else:
            cov_ref[col : col + block, row : row + block] = jnp.zeros_like(value)
        cov_ref[row : row + block, col : col + block] = value
    transposed = (((1,), (1,)), ((), ()))
    piece = data_ref.shape[0] // CHUNKS

    def dot(x, y):
        return lax.dot_general(
            x, y, transposed, precision=HIGHEST, preferred_element_type=jnp.float32
        )

    def solve_piece(start, part):
        end = start + block
        rows = slice(part * piece, (part + 1) * piece)
        solved = dot(data_ref[rows, start:end], inverse_ref[...])
        data_ref[rows, start:end] = solved
        if end < size:
            data_ref[rows, end:] = data_ref[rows, end:] - dot(solved, panel_ref[: size - end, :])
        emit(start // block, part)

    waiting = []
    for start in range(0, size, block):
        end = start + block
        work_ref[:, :block] = cov_ref[start:end, start:end]
        work_ref[:, block:] = jnp.where(r == c, 1.0, 0.0)
        for number, first in enumerate(range(0, block, PANEL)):
            eliminate_panel(work_ref, first, block)
            if waiting and number % 2 == 0:
                solve_piece(*waiting.pop(0))
        while waiting:
            solve_piece(*waiting.pop(0))
        inverse_ref[...] = work_ref[:, block:]
        if end < size:
            panel = dot(cov_ref[end:, start:end], work_ref[:, block:])
            panel_ref[: size - end, :] = panel
            cov_ref[end:, end:] = cov_ref[end:, end:] - dot(panel, panel)
        waiting = [(start, part) for part in range(CHUNKS)]
    for item in waiting:
        solve_piece(*item)


def quarter_turn(x):
    lane = lax.broadcasted_iota(jnp.int32, x.shape, 1)
    width = x.shape[1]
    return jnp.where(
        lane % 2 == 0, pltpu.roll(x, width - 1, axis=1), -pltpu.roll(x, 1, axis=1)
    )


def doppler_constants(pulses, devices, group):
    bins = pulses // devices
    lane = np.arange(bins * group)
    turn = (lane // group)[None, :] * np.arange(devices)[:, None] % pulses
    angle = turn * (2.0 * math.pi / pulses)
    first = np.arange(bins)
    phase = (first[:, None] * first[None, :] % bins) * (2.0 * math.pi / bins)
    cosine, sine = np.cos(phase), np.sin(phase)
    pair = np.stack(
        [np.stack([cosine, -sine], axis=-1), np.stack([sine, cosine], axis=-1)], axis=1
    ) / math.sqrt(pulses)
    table = np.einsum("paqb,cd->pcaqdb", pair, np.eye(group // 2))
    table = table.reshape(bins * group, bins * group)
    return tuple(np.asarray(v, np.float32) for v in (np.cos(angle), np.sin(angle), table))


def transform_chunk(rows, group, gathered_ref, const_ref, stage_ref, spread_ref):
    devices, _, width = gathered_ref.shape
    count = rows.size
    bins = width // group
    for at in range(0, width, LANES):
        lanes = slice(at, at + LANES)
        parts = [gathered_ref[z, rows, lanes] for z in range(devices)]
        turned = [quarter_turn(x) for x in parts]
        for k in range(devices):
            total = None
            for z in range(devices):
                step = z * k % devices
                for weight, term in (
                    (math.cos(2.0 * math.pi * step / devices), parts[z]),
                    (math.sin(2.0 * math.pi * step / devices), turned[z]),
                ):
                    if abs(weight) < 1e-9:
                        continue
                    sign = 1.0 if weight > 0 else -1.0
                    if abs(abs(weight) - 1.0) > 1e-9:
                        term, sign = term * weight, 1.0
                    if total is None:
                        total = term if sign > 0 else -term
                    else:
                        total = total + term if sign > 0 else total - term
            total = total * const_ref[width + k : width + k + 1, lanes] + quarter_turn(
                total
            ) * const_ref[width + devices + k : width + devices + k + 1, lanes]
            stage_ref[k * count : (k + 1) * count, lanes] = total
    mixed = jnp.dot(
        stage_ref[...], const_ref[:width, :], precision=HIGHEST, preferred_element_type=jnp.float32
    )
    place = lax.broadcasted_iota(jnp.int32, (count, LANES), 1) // group
    for target in range(devices):
        for at in range(0, width, LANES):
            out = None
            for n in range(LANES // group):
                k = target * bins + at // group + n
                low, high = k % devices, k // devices
                source = high * group
                block = source // LANES * LANES
                piece = mixed[low * count : (low + 1) * count, block : block + LANES]
                shift = (n * group - source) % LANES
                if shift:
                    piece = pltpu.roll(piece, shift, axis=1)
                out = piece if out is None else jnp.where(place == n, piece, out)
            spread_ref[target, rows, at : at + LANES] = out


def exchange(
    samples_ref, taps_ref, taper_ref, load, load_const, const_ref, snapshot_ref, low_ref, high_ref,
    padded_ref, outgoing_ref, gathered_ref, stage_ref, spread_ref, group, sems, use_part
):
    halo_send, halo_recv, in_send, in_recv, back_send, back_recv = sems
    gates, width = samples_ref.shape
    devices, share, _ = gathered_ref.shape
    half = low_ref.shape[0]
    count = share // CHUNKS
    z = lax.axis_index("pulse")
    me, ranges = lax.axis_index("range"), lax.axis_size("range")

    def send(src, dst, send_sem, recv_sem, axis, target):
        copy = pltpu.make_async_remote_copy(
            src_ref=src, dst_ref=dst, send_sem=send_sem, recv_sem=recv_sem,
            device_id={axis: target}, device_id_type=pl.DeviceIdType.MESH,
        )
        copy.start()
        return copy

    halos = [
        send(
            samples_ref.at[gates - half :], low_ref, halo_send.at[0], halo_recv.at[0],
            "range", lax.rem(me + 1, ranges),
        ),
        send(
            samples_ref.at[:half], high_ref, halo_send.at[1], halo_recv.at[1],
            "range", lax.rem(me + ranges - 1, ranges),
        ),
    ]
    tap_count = taps_ref.shape[1]
    room = -(-(tap_count + count) // LANES) * LANES
    taps = jnp.concatenate(
        [taps_ref[...], jnp.zeros((1, room - tap_count), jnp.float32)], axis=1
    )
    span = count + 2 * half
    band = pltpu.roll(
        jnp.broadcast_to(taps, (count, room)), 0, axis=1, stride=1, stride_axis=0
    )[:, :span]
    pulse = lax.broadcasted_iota(jnp.int32, (1, width), 1) // group
    taper = jnp.zeros((1, width), jnp.float32)
    for p in range(width // group):
        taper = jnp.where(pulse == p, taper_ref[p], taper)
    inner = [
        p for p in range(CHUNKS) if p * count >= half and share - (p + 1) * count >= half
    ]
    outer = [p for p in range(CHUNKS) if p not in inner]
    order = inner + outer
    shifts = sorted(range(1, devices), key=lambda s: abs(2 * s - devices))
    ins = {}
    load.wait()
    for part in order:
        if part == outer[0]:
            for copy in halos:
                copy.wait_recv()
            padded_ref[:half, :] = jnp.where(me > 0, low_ref[...], 0.0)
            padded_ref[half + gates :, :] = jnp.where(me < ranges - 1, high_ref[...], 0.0)
        for shift in shifts + [0]:
            target = lax.rem(z + shift, devices)
            start = pl.multiple_of(target * share + part * count, 8)
            value = taper * jnp.dot(
                band, padded_ref[pl.ds(start, span), :], precision=HIGHEST,
                preferred_element_type=jnp.float32,
            )
            rows = pl.ds(part * count, count)
            if shift == 0:
                gathered_ref[z, rows, :] = value
                continue
            here = outgoing_ref.at[pl.ds(start, count)]
            here[...] = value
            ins[part, shift] = send(
                here, gathered_ref.at[z, rows], in_send.at[shift - 1, part],
                in_recv.at[shift - 1, part], "pulse", target,
            )
    load_const.wait()
    backs = {}
    for part in order:
        rows = pl.ds(part * count, count)
        for shift in shifts:
            ins[part, shift].wait_recv()
        transform_chunk(rows, group, gathered_ref, const_ref, stage_ref, spread_ref)
        home = pl.ds(pl.multiple_of((part * devices + z) * count, 8), count)
        for shift in shifts:
            target = lax.rem(z + shift, devices)
            backs[part, shift] = send(
                spread_ref.at[target, rows], snapshot_ref.at[home],
                back_send.at[shift - 1, part], back_recv.at[shift - 1, part],
                "pulse", target,
            )
        snapshot_ref[home, :] = spread_ref[z, rows, :]
    for part in order:
        for shift in shifts:
            backs[part, shift].wait_recv()
        use_part(part, part == order[0])
    return halos + list(ins.values()) + list(backs.values())


def whole_kernel(
    total_gates, group, samples_ref, taps_ref, taper_ref, given_ref, out_ref,
    snapshot_ref, low_ref, high_ref, padded_ref, outgoing_ref, gathered_ref, stage_ref,
    spread_ref, const_ref, inverse_ref, panel_ref, part_ref, pair_ref, half_ref, inbox_ref,
    total_ref, cov_ref, work_ref, load_sem, const_sem, out_sem, *sems
):
    z, devices = lax.axis_index("pulse"), lax.axis_size("pulse")
    me, ranges = lax.axis_index("range"), lax.axis_size("range")
    gates, size = samples_ref.shape
    block = work_ref.shape[0]
    half = low_ref.shape[0]
    load = pltpu.make_async_copy(samples_ref, padded_ref.at[half : half + gates], load_sem)
    load.start()
    load_const = pltpu.make_async_copy(given_ref, const_ref, const_sem)
    load_const.start()
    greet(
        range_partners()
        + [("range", lax.rem(me + 1, ranges)), ("range", lax.rem(me + ranges - 1, ranges))]
        + [("pulse", lax.rem(z + shift, devices)) for shift in range(1, devices)]
    )
    piece = gates // CHUNKS

    def add_gram(part, first):
        rows = slice(part * piece, (part + 1) * piece)
        for row in range(0, size, block):
            gram = lax.dot_general(
                snapshot_ref[rows, row : row + block], snapshot_ref[rows, : row + block],
                (((0,), (0,)), ((), ())), precision=HIGHEST, preferred_element_type=jnp.float32,
            )
            for b_row, b_col, at in lower_blocks(size, block):
                if b_row == row:
                    value = gram[:, b_col : b_col + block]
                    if not first:
                        value = part_ref[at : at + block, :] + value
                    part_ref[at : at + block, :] = value

    sent = exchange(
        samples_ref, taps_ref, taper_ref, load, load_const, const_ref, snapshot_ref, low_ref,
        high_ref, padded_ref, outgoing_ref, gathered_ref, stage_ref, spread_ref, group, sems[:6],
        add_gram,
    )
    sum_over_range(part_ref, pair_ref, half_ref, inbox_ref, total_ref, sems[6:])
    written = []
    count = piece // devices

    def emit(column, part):
        cols = slice(column * block, (column + 1) * block)
        for source in range(devices):
            at = part * piece + source * count
            to = source * CHUNKS * count + part * count
            copy = pltpu.make_async_copy(
                snapshot_ref.at[at : at + count, cols], out_ref.at[to : to + count, cols],
                out_sem.at[column, part, source],
            )
            copy.start()
            written.append(copy)

    factor_and_solve(
        total_gates, total_ref, snapshot_ref, cov_ref, work_ref, inverse_ref, panel_ref, emit
    )
    for copy in sent:
        copy.wait_send()
    for copy in written:
        copy.wait()


def whiten_scratch(size, block, groups):
    packed = len(lower_blocks(size, block)) * block
    half = packed // 2
    assert half % (8 * groups) == 0
    dma = pltpu.SemaphoreType.DMA
    others = max(groups - 1, 1)
    return [
        pltpu.VMEM((packed, block), jnp.float32),
        pltpu.VMEM((half, block), jnp.float32),
        pltpu.VMEM((half, block), jnp.float32),
        pltpu.VMEM((others, half // groups, block), jnp.float32),
        pltpu.VMEM((packed, block), jnp.float32),
        pltpu.VMEM((size, size), jnp.float32),
        pltpu.VMEM((block, 2 * block), jnp.float32),
    ], [
        dma, dma, dma((others,)), dma((others,)), dma((others,)), dma((others,)),
        dma((groups,)), dma((groups,)),
    ]


def local(samples, taps, taper):
    gates, width = samples.shape
    tap_count = taps.shape[0]
    half = tap_count // 2
    bins = taper.shape[0]
    devices, ranges = lax.axis_size("pulse"), lax.axis_size("range")
    group = width // bins
    share = gates // devices
    count = share // CHUNKS
    block = min(BLOCK, width)
    cosine, sine, table = doppler_constants(bins * devices, devices, group)
    given = np.concatenate([table, cosine, sine], axis=0)
    buffers, sems = whiten_scratch(width, block, ranges // 2)
    dma = pltpu.SemaphoreType.DMA
    own = [
        pltpu.VMEM((gates, width), jnp.float32),
        pltpu.VMEM((half, width), jnp.float32),
        pltpu.VMEM((half, width), jnp.float32),
        pltpu.VMEM((gates + 2 * half, width), jnp.float32),
        pltpu.VMEM((gates, width), jnp.float32),
        pltpu.VMEM((devices, share, width), jnp.float32),
        pltpu.VMEM((devices * count, width), jnp.float32),
        pltpu.VMEM((devices, share, width), jnp.float32),
        pltpu.VMEM(given.shape, jnp.float32),
        pltpu.VMEM((block, block), jnp.float32),
        pltpu.VMEM((width, block), jnp.float32),
    ]
    pulse_sems = [dma, dma, dma((width // block, CHUNKS, devices)), dma((2,)), dma((2,))] + [dma((devices - 1, CHUNKS))] * 4
    return pl.pallas_call(
        functools.partial(whole_kernel, gates * ranges, group),
        out_shape=jax.ShapeDtypeStruct(samples.shape, jnp.float32),
        in_specs=[
            pl.BlockSpec(memory_space=pl.ANY),
            pl.BlockSpec(memory_space=pltpu.VMEM),
            pl.BlockSpec(memory_space=pltpu.SMEM),
            pl.BlockSpec(memory_space=pl.ANY),
        ],
        out_specs=pl.BlockSpec(memory_space=pl.ANY),
        scratch_shapes=own + buffers + pulse_sems + sems,
        compiler_params=pltpu.CompilerParams(
            vmem_limit_bytes=60 << 20, collective_id=1, has_side_effects=True
        ),
        name="whiten",
    )(samples, taps[None, :], taper, given)


def solution(mesh):
    placed = (P("range", "pulse"), P(), P("pulse"))
    return jax.shard_map(
        local, mesh=mesh, in_specs=placed, out_specs=P("range", "pulse"), check_vma=False
    )
```
